256 devices in a mesh: clus: 16 (over y, x), blk: 16 (over z, core).
Axes of the slice: x: 4, y: 4, z: 8, core: 2. Of those that a mesh axis runs over, the one named last changes fastest.
Arguments:
- leaf_basis: bfloat16 [2048, 256, 128], P(('clus', 'blk')), may hold values from -6 to 6
- transfer: float32 [2048, 128, 256], P(('clus', 'blk')), may hold values from -0.08 to 1.68
- block_rows: bfloat16 [4096, 256, 192], P(('clus', 'blk')), may hold values from -6 to 6
- block_cols: bfloat16 [4096, 256, 192], P(('clus', 'blk')), may hold values from -0.4375 to 0.4375
- rank_slabs: int32 [4096], P(('clus', 'blk')), may hold values from 1 to 3, as said below
- row_leaf: int32 [4096], P(('clus', 'blk')), may hold values from 0 to 127
- col_group: int32 [4096, 1], P(('clus', 'blk')), may hold values from 0 to 15; in each aligned block of 16 rows (0 to 15, 16 to 31, ...) at most 2 rows name the same one
- col_leaf: int32 [4096], P(('clus', 'blk')), may hold values from 0 to 127
Outputs:
- coupling: float32 [4096, 128, 128], P(('clus', 'blk'))
- transfer_new: float32 [2048, 128, 256], P(('clus', 'blk'))
The draws below stay inside these ranges and needn't reach their ends.
Inputs may be any that keep to these rules, and one draw needn't show every extreme that they name: `col_group`: among the 16 blocks of one device at most 2 have the same column group. `rank_slabs`: some block has 3 granules and some has one.
All inputs are finite; a program needn't handle non-finite values.
Results may differ from the reference program's by a relative error of at most 0.0058.
Values may be sent and summed in bfloat16 or wider, within the bound.
A program may use at most 128 MiB of HBM per device.

```python
import math
import jax
import jax.numpy as jnp
import numpy as np
from jax import lax

LEAF_RANK = 128
PARENT_RANK = 256
POINTS = 256
SLAB = 64
SLABS = 3
LEAF_DEV = 8
BLOCK_DEV = 16
RANK_MAX = 192
LEAVES = 2048
GROUP_LEAVES = 128
BLOCKS = 4096
CAPACITY = 2
N_CLUS = 16
N_BLK = 16


def draw_transfer(key, part):
    key_diag, key_jitter = jax.random.split(key)
    diag_gain = jnp.exp(jax.random.uniform(key_diag, (LEAVES, LEAF_RANK), jnp.float32, 0.0, jnp.log(1.6)))
    jitter = jax.random.truncated_normal(key_jitter, -3.0, 3.0, (LEAVES, LEAF_RANK, PARENT_RANK), jnp.float32)
    jitter = jitter * 0.025
    slot_index = jnp.arange(LEAVES, dtype=jnp.int32) % LEAF_DEV
    upper_half = (slot_index >= LEAF_DEV // 2).astype(jnp.int32)
    row_index = lax.broadcasted_iota(jnp.int32, (LEAVES, LEAF_RANK, PARENT_RANK), 1)
    column = lax.broadcasted_iota(jnp.int32, (LEAVES, LEAF_RANK, PARENT_RANK), 2)
    on_diag = column == row_index + upper_half[:, None, None] * LEAF_RANK
    return jitter + jnp.where(on_diag, diag_gain[:, :, None], 0.0)


def draw_rank_slabs(key, part):
    key_base, key_top, key_low = jax.random.split(key, 3)
    slab_counts = jax.random.randint(key_base, (BLOCKS,), 1, SLABS + 1, dtype=jnp.int32)
    top_at = jax.random.randint(key_top, (), 0, BLOCKS, dtype=jnp.int32)
    low_at = (top_at + jax.random.randint(key_low, (), 1, BLOCKS, dtype=jnp.int32)) % BLOCKS
    places = jnp.arange(BLOCKS, dtype=jnp.int32)
    slab_counts = jnp.where(places == top_at, SLABS, slab_counts)
    return jnp.where(places == low_at, 1, slab_counts).astype(jnp.int32)


def place_ends(entries, key, smallest, top_value):
    longest = entries.shape.index(max(entries.shape))
    spots = []
    for shift in (0, 1):
        where = [jax.random.randint(jax.random.fold_in(key, axis), (), 0, length) for axis, length in enumerate(entries.shape)]
        where[longest] = (where[longest] + shift) % entries.shape[longest]
        spots.append(tuple(where))
    return entries.at[spots[0]].set(smallest).at[spots[1]].set(top_value)


def steps_of(stream_key, extent, cuts, low, high):
    loudness = 1.0
    for position, blocks in cuts:
        steps = jax.random.uniform(jax.random.fold_in(jax.random.fold_in(stream_key, 6), position), (blocks,), jnp.float32, low / len(cuts), high / len(cuts))
        loudness = loudness * jnp.repeat(jnp.exp(steps), extent[position] // blocks).reshape((-1,) + (1,) * (len(extent) - 1 - position))
    return loudness


def assign_block(rng, own, number, rows, amount, top, reach, slope):
    sequence = jax.random.permutation(rng, amount)
    crowded, usual = portions_of(amount, rows * top, reach, slope, True), portions_of(amount, rows * top, reach, slope, False)
    places = jnp.arange(amount)

    def named(sizes, rotation):
        used = int((sizes > 0).sum())
        fixed = max(1, used // 4)
        shifted = fixed + (places - fixed + rotation * (used - fixed)) % max(1, amount - fixed)
        return jnp.zeros((amount,), jnp.int32).at[sequence[jnp.where(places < fixed, places, shifted)]].set(jnp.asarray(sizes, jnp.int32))

    sizes = jnp.where(number % 4 == 0, named(crowded, number // 4), named(usual, number - number // 4 - 1))
    mixed = jax.random.permutation(jax.random.fold_in(own, 3), amount)
    source_of, taker = mixed[0:amount // 2 * 2:2], mixed[1:amount // 2 * 2:2]
    margin = jnp.minimum(sizes[source_of] - 1, reach - sizes[taker]) // 2
    margin = jnp.where((source_of == sequence[0]) | (taker == sequence[0]) | (sizes[taker] == 0), 0, jnp.maximum(margin, 0))
    shifted = jax.random.randint(jax.random.fold_in(own, 4), (amount // 2,), 0, 1 << 20) % (margin + 1)
    sizes = sizes.at[source_of].add(-shifted).at[taker].add(shifted)
    labels = jnp.searchsorted(jnp.cumsum(sizes), jnp.arange(rows * top), side="right").astype(jnp.int32)
    grid = labels.reshape(top, rows).T
    grid = grid[jax.random.permutation(jax.random.fold_in(own, 1), rows)]
    rotation = jax.random.randint(jax.random.fold_in(own, 2), (rows, 1), 0, top)
    return jnp.take_along_axis(grid, (jnp.arange(top)[None, :] + rotation) % top, axis=1)


def portions_of(amount, total, limit, lean, full):
    loads = [(1 << 20) // math.isqrt(rank ** lean) + 1 for rank in range(1, amount + 1)]
    largest = limit if full else min(limit, max(-(-total // amount), total * loads[0] // sum(loads)))
    least = 1 if total - largest >= amount - 1 else 0
    counts, surplus = [largest] + [least] * (amount - 1), total - largest - least * (amount - 1)
    while surplus > 0:
        candidates = [i for i in range(1, amount) if counts[i] < largest] or [i for i in range(1, amount) if counts[i] < limit]
        whole, remaining = sum([loads[i] for i in candidates]), surplus
        for i in candidates:
            more = min(limit - counts[i], max(1, remaining * loads[i] // whole), surplus)
            counts[i] = counts[i] + more
            surplus = surplus - more
    return np.array(counts)


def normal_values(own_key, extent, width, bound, cuts=(), held_as=jnp.bfloat16):
    result = jax.random.normal(own_key, extent, jnp.float32) * width
    if len(cuts) > 0:
        result = steps_of(own_key, extent, cuts, -0.22, 0.18) * result
    return jnp.clip(result, min=-bound, max=bound).astype(held_as)


def setup_inputs(seed: int = 0) -> dict:
    streams_of = jax.random.split(jax.random.key(seed), 9)
    leaf_basis = normal_values(streams_of[0], (LEAVES, POINTS, LEAF_RANK), 1.0, 6.0, ((0, 256),))
    transfer = draw_transfer(jax.random.fold_in(streams_of[8], 71), 0)
    block_rows = normal_values(streams_of[2], (BLOCKS, POINTS, RANK_MAX), 1.0, 6.0, ((0, 256),))
    block_cols = normal_values(streams_of[3], (BLOCKS, POINTS, RANK_MAX), RANK_MAX ** -0.5, 0.4375, ((0, 256),))
    rank_slabs = draw_rank_slabs(jax.random.fold_in(streams_of[8], 71), 0)
    row_leaf = place_ends(jax.random.randint(streams_of[5], (BLOCKS,), 0, GROUP_LEAVES), jax.random.fold_in(streams_of[5], 1), 0, GROUP_LEAVES - 1).astype(jnp.int32)
    col_group_keys = jax.random.split(jax.random.fold_in(streams_of[6], 1), BLOCKS // BLOCK_DEV)
    col_group_turns = jax.random.permutation(jax.random.fold_in(streams_of[6], 3), BLOCKS // BLOCK_DEV)
    col_group = jax.vmap(lambda own, number: assign_block(jax.random.fold_in(streams_of[6], 2), own, number, BLOCK_DEV, N_CLUS, 1, CAPACITY, 2))(col_group_keys, col_group_turns).reshape((BLOCKS, 1))
    col_leaf = place_ends(jax.random.randint(streams_of[7], (BLOCKS,), 0, GROUP_LEAVES), jax.random.fold_in(streams_of[7], 1), 0, GROUP_LEAVES - 1).astype(jnp.int32)
    return {"leaf_basis": leaf_basis, "transfer": transfer, "block_rows": block_rows, "block_cols": block_cols, "rank_slabs": rank_slabs, "row_leaf": row_leaf, "col_group": col_group, "col_leaf": col_leaf}


def reference(leaf_basis, transfer, block_rows, block_cols, rank_slabs, row_leaf, col_group, col_leaf):
    leaf_float = leaf_basis.astype(jnp.float32)
    gram_leaf = jnp.einsum('npk,npq->nkq', leaf_float, leaf_float, precision=lax.Precision.HIGHEST)
    lower_leaf = jnp.linalg.cholesky(gram_leaf)
    basis_rows = jax.scipy.linalg.solve_triangular(lower_leaf, jnp.swapaxes(leaf_float, 1, 2), lower=True)
    basis_rows = basis_rows.astype(jnp.bfloat16)
    stacked = jnp.einsum('nqk,nqj->nkj', lower_leaf, transfer, precision=lax.Precision.HIGHEST)
    devices = LEAVES // LEAF_DEV
    half_count = LEAF_DEV // 2
    per_device = stacked.reshape(devices, LEAF_DEV, LEAF_RANK, PARENT_RANK)
    partner = per_device.reshape(devices // 2, 2, LEAF_DEV, LEAF_RANK, PARENT_RANK)[:, ::-1].reshape(per_device.shape)
    first_child = per_device[:, :half_count]
    second_child = partner[:, half_count:]
    gram_parent = jnp.einsum('dmkj,dmki->dmji', first_child, first_child, precision=lax.Precision.HIGHEST)
    gram_parent = gram_parent + jnp.einsum('dmkj,dmki->dmji', second_child, second_child, precision=lax.Precision.HIGHEST)
    lower_parent = jnp.linalg.cholesky(gram_parent)
    swapped = lower_parent.reshape(devices // 2, 2, half_count, PARENT_RANK, PARENT_RANK)[:, ::-1].reshape(lower_parent.shape)
    lower_all = jnp.concatenate([lower_parent, swapped], axis=1)
    new_rows = jax.scipy.linalg.solve_triangular(lower_all, jnp.swapaxes(per_device, 2, 3), lower=True)
    transfer_new = jnp.swapaxes(new_rows, 2, 3).reshape(LEAVES, LEAF_RANK, PARENT_RANK)
    block_ids = jnp.arange(BLOCKS, dtype=jnp.int32)
    row_cluster = (block_ids // (BLOCK_DEV * N_BLK) * GROUP_LEAVES + row_leaf).astype(jnp.int32)
    col_cluster = (col_group[:, 0] * GROUP_LEAVES + col_leaf).astype(jnp.int32)
    widths = (rank_slabs * SLAB).astype(jnp.int32)
    batches = BLOCKS // BLOCK_DEV

    def one_batch(pieces):
        rows_part, cols_part, row_ids, col_ids, width_part = pieces
        live_cols = jnp.arange(RANK_MAX, dtype=jnp.int32)[None, None, :] < width_part[:, None, None]
        rows_live = jnp.where(live_cols, rows_part, jnp.zeros_like(rows_part)).astype(jnp.float32)
        cols_live = jnp.where(live_cols, cols_part, jnp.zeros_like(cols_part)).astype(jnp.float32)
        row_basis = basis_rows[row_ids].astype(jnp.float32)
        col_basis = basis_rows[col_ids].astype(jnp.float32)
        near_proj = jnp.einsum('bkp,bpr->bkr', row_basis, rows_live, precision=lax.Precision.HIGHEST).astype(jnp.bfloat16)
        far_proj = jnp.einsum('bkp,bpr->bkr', col_basis, cols_live, precision=lax.Precision.HIGHEST).astype(jnp.bfloat16)
        near_proj = lax.optimization_barrier(near_proj)
        far_proj = lax.optimization_barrier(far_proj)
        return jnp.einsum('bkr,bjr->bkj', near_proj.astype(jnp.float32), far_proj.astype(jnp.float32), precision=lax.Precision.HIGHEST)
    coupling = lax.map(one_batch, (block_rows.reshape(batches, BLOCK_DEV, POINTS, RANK_MAX), block_cols.reshape(batches, BLOCK_DEV, POINTS, RANK_MAX), row_cluster.reshape(batches, BLOCK_DEV), col_cluster.reshape(batches, BLOCK_DEV), widths.reshape(batches, BLOCK_DEV)))
    coupling = coupling.reshape(BLOCKS, LEAF_RANK, LEAF_RANK)
    return (coupling, transfer_new)
```

```python
import functools

import jax
import jax.numpy as jnp
from jax import lax
from jax.experimental import pallas as pl
from jax.experimental.pallas import tpu as pltpu
from jax.sharding import PartitionSpec as P

SLAB = 64
F32, BF16 = jnp.float32, jnp.bfloat16
BATCH = 8
PANEL = 8


def split2(x):
    hi = x.astype(BF16)
    return hi, (x - hi.astype(F32)).astype(BF16)


def dot(a, b, ca, cb):
    return lax.dot_general(a, b, (((ca,), (cb,)), ((), ())), preferred_element_type=F32)


def lane(row, j):
    part = row[j // 128]
    return jnp.broadcast_to(part[:, j % 128 : j % 128 + 1], (BATCH, 128))


def factor_block(rows, first, live):
    count = len(rows)
    for base in range(0, count, PANEL):
        s = {}
        for i in range(PANEL):
            for j in range(i, PANEL):
                s[i, j] = lane(rows[base + i], first + base + j)
        for k in range(PANEL):
            d = lax.rsqrt(s[k, k])
            for j in range(k + 1, PANEL):
                s[k, j] = s[k, j] * d
            for i in range(k + 1, PANEL):
                for j in range(i, PANEL):
                    s[i, j] = s[i, j] - s[k, i] * s[k, j]
            rows[base + k] = {t: v * d for t, v in rows[base + k].items()}
            for i in range(k + 1, PANEL):
                rows[base + i] = {
                    t: v - s[k, i] * rows[base + k][t] for t, v in rows[base + i].items()
                }
        for i in range(base + PANEL, count):
            row = dict(rows[i])
            for k in range(PANEL):
                m = lane(rows[base + k], first + i)
                for t in row:
                    row[t] = row[t] - m * rows[base + k][t]
            rows[i] = row
    return rows


def columns(work, span, start, count):
    return jnp.concatenate([work[t, start : start + count, :] for t in span], axis=1)


def put(work, first, start, value):
    for t in range(value.shape[1] // 128):
        work[first + t, start : start + value.shape[0], :] = value[:, t * 128 : (t + 1) * 128]


def factor(work, n, nb):
    tiles = n // 128
    for first in range(0, n, nb):
        t0 = first // 128
        live = list(range(t0, tiles)) + [tiles + t for t in range(t0 + 1)]
        rows = []
        for i in range(first, first + nb):
            rows.append({t: work[t, pl.ds(i, BATCH, stride=n), :] for t in live})
        rows = factor_block(rows, first, live)
        for i in range(nb):
            for t in live:
                work[t, pl.ds(first + i, BATCH, stride=n), :] = rows[i][t]
        rest = first + nb
        if rest < n:
            r0 = rest // 128
            span = list(range(r0, tiles)) + [tiles + t for t in range(t0 + 1)]
            skip = rest - r0 * 128
            for m in range(BATCH):
                hi, lo = split2(columns(work, span, m * n + first, nb))
                lhs = jnp.concatenate([hi, lo, hi], axis=0)[:, 0 : n - r0 * 128]
                rhs = jnp.concatenate([hi, hi, lo], axis=0)
                upd = dot(lhs, rhs, 0, 0)
                for at, t in enumerate(span):
                    work[t, m * n + rest : (m + 1) * n, :] = (
                        work[t, m * n + rest : (m + 1) * n, :] - upd[skip:, at * 128 : (at + 1) * 128]
                    )


def eye(n):
    return (lax.broadcasted_iota(jnp.int32, (n, n), 0) == lax.broadcasted_iota(jnp.int32, (n, n), 1)).astype(F32)


def upper(x):
    n = x.shape[0]
    return jnp.where(
        lax.broadcasted_iota(jnp.int32, (n, n), 0) <= lax.broadcasted_iota(jnp.int32, (n, n), 1), x, 0.0
    )


def leaf_kernel(a_ref, t_ref, basis_ref, s_ref, s16_ref, work, *, nb):
    n = a_ref.shape[2]
    for m in range(BATCH):
        a = a_ref[m]
        put(work, 0, m * n, dot(a, a, 0, 0))
        put(work, n // 128, m * n, eye(n))
    factor(work, n, nb)
    for m in range(BATCH):
        u = upper(columns(work, range(n // 128), m * n, n))
        x = columns(work, range(n // 128, n // 64), m * n, n)
        xh, xl = split2(x)
        a = a_ref[m]
        basis_ref[m] = (dot(xh, a, 1, 1) + dot(xl, a, 1, 1)).astype(BF16)
        uh, ul = split2(u)
        th, tl = split2(t_ref[m])
        lhs = jnp.concatenate([uh, ul], axis=1)
        st = dot(lhs, jnp.concatenate([th, th], axis=0), 1, 0) + dot(uh, tl, 1, 0)
        s_ref[m] = st
        s16_ref[m] = st.astype(BF16)


def parent_kernel(s_ref, p_ref, new_ref, work, *, nb):
    n = s_ref.shape[2]
    for m in range(BATCH):
        sh, sl = split2(s_ref[m])
        p = p_ref[(m + BATCH // 2) % BATCH]
        g = dot(jnp.concatenate([sh, sl], axis=0), jnp.concatenate([sh, sh], axis=0), 0, 0)
        g = g + dot(jnp.concatenate([sh, p], axis=0), jnp.concatenate([sl, p], axis=0), 0, 0)
        put(work, 0, m * n, g)
        put(work, n // 128, m * n, eye(n))
    factor(work, n, nb)
    for m in range(BATCH):
        sh, sl = split2(s_ref[m])
        xh, xl = split2(columns(work, range(n // 128, n // 64), m * n, n))
        new_ref[m] = dot(sh, xh, 1, 1) + (dot(sh, xl, 1, 1) + dot(sl, xh, 1, 1))


def leaf(a, t, nb=32):
    n = a.shape[2]
    return pl.pallas_call(
        functools.partial(leaf_kernel, nb=nb),
        out_shape=(
            jax.ShapeDtypeStruct((8, n, 256), BF16),
            jax.ShapeDtypeStruct((8, n, 256), F32),
            jax.ShapeDtypeStruct((8, n, 256), BF16),
        ),
        in_specs=[pl.BlockSpec(memory_space=pltpu.VMEM)] * 2,
        out_specs=[pl.BlockSpec(memory_space=pltpu.VMEM)] * 3,
        scratch_shapes=[pltpu.VMEM((2 * n // 128, 8 * n, 128), F32)],
        name="leaf",
    )(a, t)


def parent(s, p, nb=32):
    n = s.shape[2]
    return pl.pallas_call(
        functools.partial(parent_kernel, nb=nb),
        out_shape=jax.ShapeDtypeStruct(s.shape, F32),
        in_specs=[pl.BlockSpec(memory_space=pltpu.VMEM)] * 2,
        out_specs=pl.BlockSpec(memory_space=pltpu.VMEM),
        scratch_shapes=[pltpu.VMEM((2 * n // 128, 8 * n, 128), F32)],
        name="parent",
    )(s, p)


def block_kernel(row_leaf, slot_of, rank, row_basis, col_basis, rows, cols, out):
    b = pl.program_id(0)
    near = dot(row_basis[0], rows[0], 1, 0)
    live = lax.broadcasted_iota(jnp.int32, near.shape, 1) < rank[b] * SLAB
    near = jnp.where(live, near, 0.0).astype(BF16)
    far = dot(col_basis[0], cols[0], 1, 0).astype(BF16)
    out[0] = dot(near, far, 1, 1)


def couple(row_leaf, slot_of, rank, gathered, slots, rows, cols):
    count, points, rank_max = rows.shape
    k = gathered.shape[1]
    return pl.pallas_call(
        block_kernel,
        out_shape=jax.ShapeDtypeStruct((count, k, k), F32),
        grid_spec=pltpu.PrefetchScalarGridSpec(
            num_scalar_prefetch=3,
            grid=(count,),
            in_specs=[
                pl.BlockSpec((1, k, points), lambda b, r, s, n: (r[b], 0, 0)),
                pl.BlockSpec((1, k, points), lambda b, r, s, n: (s[b], 0, 0)),
                pl.BlockSpec((1, points, rank_max), lambda b, r, s, n: (b, 0, 0)),
                pl.BlockSpec((1, points, rank_max), lambda b, r, s, n: (b, 0, 0)),
            ],
            out_specs=pl.BlockSpec((1, k, k), lambda b, r, s, n: (b, 0, 0)),
        ),
        name="couple",
    )(row_leaf, slot_of, rank, gathered, slots, rows, cols)


def from_partner(value, axis, bit):
    mask = 2**bit
    pairs = [(source, source ^ mask) for source in range(lax.axis_size(axis))]
    return lax.ppermute(value, axis, pairs)


def per_device(
    leaf_basis, transfer, block_rows, block_cols, rank_slabs, row_leaf, col_group, col_leaf
):
    block_count, _, rank_max = block_rows.shape
    groups = lax.axis_size("clus")
    capacity = max(2, 2 * block_count // groups)
    slot_count = groups * capacity
    target = col_group[:, 0]
    member = (target[:, None] == jnp.arange(groups, dtype=jnp.int32)[None, :]).astype(jnp.int32)
    earlier = jnp.cumsum(member, axis=0) - member
    position = jnp.sum(earlier * member, axis=1)
    slot_of = target * capacity + position
    matches = (slot_of[None, :] == jnp.arange(slot_count, dtype=jnp.int32)[:, None]).astype(
        jnp.int32
    )
    wanted = jnp.sum(matches * col_leaf[None, :], axis=1).reshape(groups, capacity)
    asked = lax.all_to_all(wanted, "clus", split_axis=0, concat_axis=0, tiled=True)
    basis_rows, stacked, stacked_half = leaf(leaf_basis, transfer)
    gathered = lax.all_gather(basis_rows, "blk", axis=0, tiled=True)
    partner = from_partner(stacked_half, "blk", 0)
    transfer_new = parent(stacked, partner)
    served = jnp.take(gathered, asked, axis=0, mode="clip")
    slots = lax.all_to_all(served, "clus", split_axis=0, concat_axis=0, tiled=True)
    slots = slots.reshape(slot_count, *slots.shape[2:])
    coupling = couple(row_leaf, slot_of, rank_slabs, gathered, slots, block_rows, block_cols)
    return (coupling, transfer_new)


def solution(mesh):
    placed = (
        P(("clus", "blk"), None, None),
        P(("clus", "blk"), None, None),
        P(("clus", "blk"), None, None),
        P(("clus", "blk"), None, None),
        P(("clus", "blk")),
        P(("clus", "blk")),
        P(("clus", "blk"), None),
        P(("clus", "blk")),
    )
    return jax.shard_map(
        per_device,
        mesh=mesh,
        in_specs=placed,
        out_specs=(P(("clus", "blk"), None, None), P(("clus", "blk"), None, None)),
        check_vma=False,
    )
```

```python
import jax
import jax.numpy as jnp
from jax import lax
from jax.experimental import pallas as pl
from jax.experimental.pallas import tpu as pltpu
from jax.sharding import PartitionSpec as P

SLAB = 64
F32, BF16 = jnp.float32, jnp.bfloat16
BATCH = 8
PANEL = 8


def split2(x):
    hi = x.astype(BF16)
    return hi, (x - hi.astype(F32)).astype(BF16)


def dot(a, b, ca, cb):
    return lax.dot_general(a, b, (((ca,), (cb,)), ((), ())), preferred_element_type=F32)


def lane(row, j):
    part = row[j // 128]
    return jnp.broadcast_to(part[:, j % 128 : j % 128 + 1], (BATCH, 128))


def factor_block(rows, first, live):
    count = len(rows)
    for base in range(0, count, PANEL):
        s = {}
        for i in range(PANEL):
            for j in range(i, PANEL):
                s[i, j] = lane(rows[base + i], first + base + j)
        for k in range(PANEL):
            d = lax.rsqrt(s[k, k])
            for j in range(k + 1, PANEL):
                s[k, j] = s[k, j] * d
            for i in range(k + 1, PANEL):
                for j in range(i, PANEL):
                    s[i, j] = s[i, j] - s[k, i] * s[k, j]
            rows[base + k] = {t: v * d for t, v in rows[base + k].items()}
            for i in range(k + 1, PANEL):
                rows[base + i] = {
                    t: v - s[k, i] * rows[base + k][t] for t, v in rows[base + i].items()
                }
        for i in range(base + PANEL, count):
            row = dict(rows[i])
            for k in range(PANEL):
                m = lane(rows[base + k], first + i)
                for t in row:
                    row[t] = row[t] - m * rows[base + k][t]
            rows[i] = row
    return rows


def columns(work, span, start, count):
    return jnp.concatenate([work[t, start : start + count, :] for t in span], axis=1)


def put(work, first, start, value):
    for t in range(value.shape[1] // 128):
        work[first + t, start : start + value.shape[0], :] = value[:, t * 128 : (t + 1) * 128]


def factor(work, n, nb, after_block=None):
    tiles = n // 128
    for first in range(0, n, nb):
        t0 = first // 128
        live = list(range(t0, tiles)) + [tiles + t for t in range(t0 + 1)]
        rows = []
        for i in range(first, first + nb):
            rows.append({t: work[t, pl.ds(i, BATCH, stride=n), :] for t in live})
        rows = factor_block(rows, first, live)
        for i in range(nb):
            for t in live:
                work[t, pl.ds(first + i, BATCH, stride=n), :] = rows[i][t]
        if after_block is not None:
            after_block(first // nb)
        rest = first + nb
        if rest < n:
            r0 = rest // 128
            span = list(range(r0, tiles)) + [tiles + t for t in range(t0 + 1)]
            skip = rest - r0 * 128
            for m in range(BATCH):
                hi, lo = split2(columns(work, span, m * n + first, nb))
                lhs = jnp.concatenate([hi, lo, hi], axis=0)[:, 0 : n - r0 * 128]
                rhs = jnp.concatenate([hi, hi, lo], axis=0)
                upd = dot(lhs, rhs, 0, 0)
                for at, t in enumerate(span):
                    work[t, m * n + rest : (m + 1) * n, :] = (
                        work[t, m * n + rest : (m + 1) * n, :] - upd[skip:, at * 128 : (at + 1) * 128]
                    )


def eye(n):
    return (lax.broadcasted_iota(jnp.int32, (n, n), 0) == lax.broadcasted_iota(jnp.int32, (n, n), 1)).astype(F32)


def upper(x):
    n = x.shape[0]
    return jnp.where(
        lax.broadcasted_iota(jnp.int32, (n, n), 0) <= lax.broadcasted_iota(jnp.int32, (n, n), 1), x, 0.0
    )


MESH = pl.DeviceIdType.MESH
HALVES = 2
HOPS = 4


def remote(src, dst, send, recv, where):
    return pltpu.make_async_remote_copy(
        src_ref=src, dst_ref=dst, send_sem=send, recv_sem=recv, device_id=where, device_id_type=MESH
    )


def whole_kernel(
    row_leaf, target, position, rank,
    a_ref, t_ref, want_ref, rows_hbm, cols_hbm,
    out_ref, new_ref,
    work_leaf, work_parent, basis, stacked, stacked_send, stacked_recv, serve, slots,
    rows, cols, near, asked_v, asked,
    ring_send, ring_recv, pair_send, pair_recv, stack_sem, ask_send, ask_recv, slot_send, slot_recv,
    local_sem,
):
    clus, blk = lax.axis_index("clus"), lax.axis_index("blk")
    groups, width = lax.axis_size("clus"), lax.axis_size("blk")
    chips = width // 2
    core, chip = lax.rem(blk, 2), lax.div(blk, 2)
    right = {"blk": lax.rem(chip + 1, chips) * 2 + core}
    left = {"blk": lax.rem(chip + chips - 1, chips) * 2 + core}
    partner = {"blk": chip * 2 + 1 - core}
    n, points = a_ref.shape[2], a_ref.shape[1]
    own = blk * BATCH
    blocks = rows_hbm.shape[0]

    fetch_rows = pltpu.make_async_copy(rows_hbm, rows, local_sem.at[0])
    fetch_cols = pltpu.make_async_copy(cols_hbm, cols, local_sem.at[1])
    fetch_rows.start()
    fetch_cols.start()

    barrier = pltpu.get_barrier_semaphore()
    for where in (right, left, partner):
        pl.semaphore_signal(barrier, inc=1, device_id=where, device_id_type=MESH)

    def greet(k, carry):
        pl.semaphore_signal(
            barrier, inc=1, device_id={"clus": clus ^ k}, device_id_type=MESH
        )
        return carry

    lax.fori_loop(1, groups, greet, 0)

    for m in range(BATCH):
        a = a_ref[m]
        put(work_leaf, 0, m * n, dot(a, a, 0, 0))
        put(work_leaf, n // 128, m * n, eye(n))
    factor(work_leaf, n, 32)
    for m in range(BATCH):
        xh, xl = split2(columns(work_leaf, [1], m * n, n))
        a = a_ref[m]
        b = (dot(xh, a, 1, 1) + dot(xl, a, 1, 1)).astype(BF16)
        for h in range(HALVES):
            basis[h, own + m] = b[:, h * 128 : (h + 1) * 128]

    pl.semaphore_wait(barrier, groups + 2)

    def ask(k):
        return remote(
            want_ref.at[clus ^ k], asked_v.at[clus], ask_send.at[k], ask_recv.at[k], {"clus": clus ^ k}
        )

    def shard(z, h, c):
        return basis.at[h, pl.ds((z * 2 + c) * BATCH, BATCH)]

    def ring(side, hop, h, arriving):
        gone = hop if arriving else hop - 1
        z = lax.rem(chip + (chips - gone if side == 0 else gone), chips)
        i = side * 8 + (hop - 1) * 2 + h
        return remote(
            shard(z, h, core), shard(z, h, core), ring_send.at[i], ring_recv.at[i],
            right if side == 0 else left,
        )

    def pair(side, hop, h, arriving):
        z = lax.rem(chip + (chips - hop if side == 0 else hop), chips)
        i = side * 8 + (hop - 1) * 2 + h if hop else 16 + h
        c = 1 - core if arriving else core
        return remote(shard(z, h, c), shard(z, h, c), pair_send.at[i], pair_recv.at[i], partner)

    def travels(side, hop, h):
        return hop < HOPS or h == side

    items = [(hop, h, side) for hop in range(1, HOPS + 1) for h in range(HALVES) for side in range(2)]
    items = [x for x in items if travels(x[2], x[0], x[1])]

    for h in range(HALVES):
        for side in range(2):
            ring(side, 1, h, False).start()
        pair(0, 0, h, False).start()

    def advance(item):
        hop, h, side = item
        ring(side, hop, h, True).wait_recv()
        if hop < HOPS and travels(side, hop + 1, h):
            ring(side, hop + 1, h, False).start()
        pair(side, hop, h, False).start()

    for m in range(BATCH):
        uh, ul = split2(upper(columns(work_leaf, [0], m * n, n)))
        th, tl = split2(t_ref[m])
        st = dot(jnp.concatenate([uh, ul], axis=1), jnp.concatenate([th, th], axis=0), 1, 0)
        st = st + dot(uh, tl, 1, 0)
        stacked[m] = st
        stacked_send[m] = st.astype(BF16)
    swap = remote(stacked_send, stacked_recv, stack_sem.at[0], stack_sem.at[1], partner)
    swap.start()
    mine = pltpu.make_async_copy(want_ref.at[clus], asked_v.at[clus], local_sem.at[2])
    mine.start()

    def start_ask(k, carry):
        ask(k).start()
        return carry

    lax.fori_loop(1, groups, start_ask, 0)

    n2 = 2 * n
    swap.wait_recv()
    for m in range(BATCH):
        sh, sl = split2(stacked[m])
        p = stacked_recv[(m + BATCH // 2) % BATCH]
        g = dot(jnp.concatenate([sh, sl], axis=0), jnp.concatenate([sh, sh], axis=0), 0, 0)
        g = g + dot(jnp.concatenate([sh, p], axis=0), jnp.concatenate([sl, p], axis=0), 0, 0)
        put(work_parent, 0, m * n2, g)
        put(work_parent, n2 // 128, m * n2, eye(n2))
    pending = list(items)

    def after_block(number):
        if number in (1, 4, 7):
            advance(pending.pop(0))
            advance(pending.pop(0))

    factor(work_parent, n2, 32, after_block)
    for m in range(BATCH):
        sh, sl = split2(stacked[m])
        xh, xl = split2(columns(work_parent, range(2, 4), m * n2, n2))
        new_ref[m] = dot(sh, xh, 1, 1) + (dot(sh, xl, 1, 1) + dot(sl, xh, 1, 1))

    mine.wait()

    def end_ask(k, carry):
        ask(k).wait_recv()
        return carry

    lax.fori_loop(1, groups, end_ask, 0)
    learn = pltpu.make_async_copy(asked_v, asked, local_sem.at[3])
    learn.start()
    while pending:
        advance(pending.pop(0))
    learn.wait()
    for h in range(HALVES):
        pair(0, 0, h, True).wait_recv()
    for hop, h, side in items:
        pair(side, hop, h, True).wait_recv()

    def slot_copy(k, h):
        return remote(
            serve.at[h, k], slots.at[h, clus], slot_send.at[h, k], slot_recv.at[h, k], {"clus": clus ^ k}
        )

    def give(k, carry):
        for h in range(HALVES):
            for c in range(2):
                serve[h, k, c] = basis[h, asked[clus ^ k, 0, c]]
            slot_copy(k, h).start()
        return carry

    lax.fori_loop(1, groups, give, 0)
    for h in range(HALVES):
        for c in range(2):
            slots[h, clus, c] = basis[h, asked[clus, 0, c]]

    fetch_rows.wait()
    fetch_cols.wait()

    def near_step(i, carry):
        for j in range(4):
            b = i * 4 + j
            r = row_leaf[b]
            lhs = jnp.concatenate([basis[0, r], basis[1, r]], axis=1)
            value = dot(lhs, rows[b], 1, 1)
            live = lax.broadcasted_iota(jnp.int32, value.shape, 1) < rank[b] * SLAB
            near[b] = jnp.where(live, value, 0.0).astype(BF16)
        return carry

    lax.fori_loop(0, blocks // 4, near_step, 0)

    def take(k, carry):
        for h in range(HALVES):
            slot_copy(k, h).wait_recv()
        return carry

    lax.fori_loop(1, groups, take, 0)

    def far_step(i, carry):
        for j in range(4):
            b = i * 4 + j
            g, c = target[b], position[b]
            lhs = jnp.concatenate([slots[0, g, c], slots[1, g, c]], axis=1)
            far = dot(lhs, cols[b], 1, 1).astype(BF16)
            out_ref[b] = dot(near[b], far, 1, 1)
        return carry

    lax.fori_loop(0, blocks // 4, far_step, 0)

    for h in range(HALVES):
        for side in range(2):
            ring(side, 1, h, False).wait_send()
        pair(0, 0, h, False).wait_send()
    for hop, h, side in items:
        pair(side, hop, h, False).wait_send()
        if hop < HOPS and travels(side, hop + 1, h):
            ring(side, hop + 1, h, False).wait_send()
    swap.wait_send()

    def drain(k, carry):
        ask(k).wait_send()
        for h in range(HALVES):
            slot_copy(k, h).wait_send()
        return carry

    lax.fori_loop(1, groups, drain, 0)


def whole(row_leaf, target, position, rank, leaf_basis, transfer, want, rows, cols):
    groups, width = lax.axis_size("clus"), lax.axis_size("blk")
    count, points, n = leaf_basis.shape
    blocks, rank_max = rows.shape[0], rows.shape[1]
    smem, vmem = pltpu.SMEM, pltpu.VMEM
    dma = pltpu.SemaphoreType.DMA
    leaves = count * width
    return pl.pallas_call(
        whole_kernel,
        out_shape=(
            jax.ShapeDtypeStruct((blocks, n, n), F32),
            jax.ShapeDtypeStruct(transfer.shape, F32),
        ),
        in_specs=[pl.BlockSpec(memory_space=smem)] * 4
        + [pl.BlockSpec(memory_space=vmem)] * 3
        + [pl.BlockSpec(memory_space=pl.ANY)] * 2,
        out_specs=(pl.BlockSpec(memory_space=vmem), pl.BlockSpec(memory_space=vmem)),
        scratch_shapes=[
            vmem((2, count * n, 128), F32),
            vmem((4, count * 2 * n, 128), F32),
            vmem((HALVES, leaves, n, 128), BF16),
            vmem(transfer.shape, F32),
            vmem(transfer.shape, BF16),
            vmem(transfer.shape, BF16),
            vmem((HALVES, groups, 2, n, 128), BF16),
            vmem((HALVES, groups, 2, n, 128), BF16),
            vmem(rows.shape, BF16),
            vmem(cols.shape, BF16),
            vmem((blocks, n, rank_max), BF16),
            vmem((groups, 1, 128), jnp.int32),
            smem((groups, 1, 128), jnp.int32),
            dma((16,)),
            dma((16,)),
            dma((18,)),
            dma((18,)),
            dma((2,)),
            dma((groups,)),
            dma((groups,)),
            dma((HALVES, groups)),
            dma((HALVES, groups)),
            dma((4,)),
        ],
        compiler_params=pltpu.CompilerParams(
            collective_id=0, has_side_effects=True, vmem_limit_bytes=60 * 2**20
        ),
        name="whole",
    )(row_leaf, target, position, rank, leaf_basis, transfer, want, rows, cols)


def per_device(
    leaf_basis, transfer, block_rows, block_cols, rank_slabs, row_leaf, col_group, col_leaf
):
    groups = lax.axis_size("clus")
    target = col_group[:, 0]
    member = (target[:, None] == jnp.arange(groups, dtype=jnp.int32)[None, :]).astype(jnp.int32)
    earlier = jnp.cumsum(member, axis=0) - member
    position = jnp.sum(earlier * member, axis=1)
    picks = member[:, :, None] * (
        position[:, None, None] == jnp.arange(128, dtype=jnp.int32)[None, None, :]
    ).astype(jnp.int32)
    want = jnp.sum(picks * col_leaf[:, None, None], axis=0)[:, None, :]
    return whole(
        row_leaf,
        target,
        position,
        rank_slabs,
        leaf_basis,
        transfer,
        want,
        jnp.swapaxes(block_rows, 1, 2),
        jnp.swapaxes(block_cols, 1, 2),
    )


def solution(mesh):
    placed = (
        P(("clus", "blk"), None, None),
        P(("clus", "blk"), None, None),
        P(("clus", "blk"), None, None),
        P(("clus", "blk"), None, None),
        P(("clus", "blk")),
        P(("clus", "blk")),
        P(("clus", "blk"), None),
        P(("clus", "blk")),
    )
    return jax.shard_map(
        per_device,
        mesh=mesh,
        in_specs=placed,
        out_specs=(P(("clus", "blk"), None, None), P(("clus", "blk"), None, None)),
        check_vma=False,
    )
```

```python
import jax
import jax.numpy as jnp
from jax import lax
from jax.experimental import pallas as pl
from jax.experimental.pallas import tpu as pltpu
from jax.sharding import PartitionSpec as P

SLAB = 64
F32, BF16 = jnp.float32, jnp.bfloat16
BATCH = 8
PANEL = 8


def split2(x):
    hi = x.astype(BF16)
    return hi, (x - hi.astype(F32)).astype(BF16)


def dot(a, b, ca, cb):
    return lax.dot_general(a, b, (((ca,), (cb,)), ((), ())), preferred_element_type=F32)


def lane(row, j):
    part = row[j // 128]
    return jnp.broadcast_to(part[:, j % 128 : j % 128 + 1], (BATCH, 128))


def factor_block(rows, first, tick):
    count = len(rows)
    for base in range(0, count, PANEL):
        s = {}
        for i in range(PANEL):
            for j in range(i, PANEL):
                s[i, j] = lane(rows[base + i], first + base + j)
        for k in range(PANEL):
            d = lax.rsqrt(s[k, k])
            for j in range(k + 1, PANEL):
                s[k, j] = s[k, j] * d
            for i in range(k + 1, PANEL):
                for j in range(i, PANEL):
                    s[i, j] = s[i, j] - s[k, i] * s[k, j]
            rows[base + k] = {t: v * d for t, v in rows[base + k].items()}
            for i in range(k + 1, PANEL):
                rows[base + i] = {
                    t: v - s[k, i] * rows[base + k][t] for t, v in rows[base + i].items()
                }
        for i in range(base + PANEL, count):
            row = dict(rows[i])
            for k in range(PANEL):
                m = lane(rows[base + k], first + i)
                for t in row:
                    row[t] = row[t] - m * rows[base + k][t]
            rows[i] = row
        tick()
    return rows


def columns(work, span, start, count):
    return jnp.concatenate([work[t, start : start + count, :] for t in span], axis=1)


def put(work, first, start, value):
    for t in range(value.shape[1] // 128):
        work[first + t, start : start + value.shape[0], :] = value[:, t * 128 : (t + 1) * 128]


def factor(work, n, nb, tick, after_block):
    tiles = n // 128
    for first in range(0, n, nb):
        t0 = first // 128
        live = list(range(t0, tiles)) + [tiles + t for t in range(t0 + 1)]
        rows = []
        for i in range(first, first + nb):
            rows.append({t: work[t, pl.ds(i, BATCH, stride=n), :] for t in live})
        rows = factor_block(rows, first, tick)
        for i in range(nb):
            for t in live:
                work[t, pl.ds(first + i, BATCH, stride=n), :] = rows[i][t]
        after_block(first // nb)
        rest = first + nb
        if rest < n:
            r0 = rest // 128
            span = list(range(r0, tiles)) + [tiles + t for t in range(t0 + 1)]
            skip = rest - r0 * 128
            for m in range(BATCH):
                hi, lo = split2(columns(work, span, m * n + first, nb))
                lhs = jnp.concatenate([hi, lo, hi], axis=0)[:, 0 : n - r0 * 128]
                rhs = jnp.concatenate([hi, hi, lo], axis=0)
                upd = dot(lhs, rhs, 0, 0)
                for at, t in enumerate(span):
                    work[t, m * n + rest : (m + 1) * n, :] = (
                        work[t, m * n + rest : (m + 1) * n, :] - upd[skip:, at * 128 : (at + 1) * 128]
                    )


def eye(n):
    return (lax.broadcasted_iota(jnp.int32, (n, n), 0) == lax.broadcasted_iota(jnp.int32, (n, n), 1)).astype(F32)


def upper(x):
    n = x.shape[0]
    return jnp.where(
        lax.broadcasted_iota(jnp.int32, (n, n), 0) <= lax.broadcasted_iota(jnp.int32, (n, n), 1), x, 0.0
    )


MESH = pl.DeviceIdType.MESH
PARTS = 4
SUBS = 2
HOPS = 4
LEAF_TICK, PARENT_TICK = 0.5, 0.48
HOP_US, FIRST_US = 0.7, 0.8
GROUP = 2
FINISH = 2


def remote(src, dst, send, recv, where):
    return pltpu.make_async_remote_copy(
        src_ref=src, dst_ref=dst, send_sem=send, recv_sem=recv, device_id=where, device_id_type=MESH
    )


def loop(low, high, step):
    def body(i, carry):
        step(i)
        return carry

    lax.fori_loop(low, high, body, 0)


def whole_kernel(
    row_leaf, target, col_leaf, rank,
    a_ref, t_hbm, rows_hbm, cols_hbm,
    out_ref, new_ref,
    work_leaf, work_parent, stacked, stacked_send, stacked_recv, serve,
    t_ref, rows, cols, near, want, asked_v, asked, position,
    ring_send, ring_recv, pair_send, pair_recv, stack_sem, ask_send, ask_recv, slot_send, slot_recv,
    local_sem, *parted,
):
    basis, slots = parted[:PARTS], parted[PARTS:]
    clus, blk = lax.axis_index("clus"), lax.axis_index("blk")
    groups, width = lax.axis_size("clus"), lax.axis_size("blk")
    chips = width // 2
    core, chip = lax.rem(blk, 2), lax.div(blk, 2)
    sides = (
        {"blk": lax.rem(chip + 1, chips) * 2 + core},
        {"blk": lax.rem(chip + chips - 1, chips) * 2 + core},
    )
    partner = {"blk": chip * 2 + 1 - core}
    n = a_ref.shape[2]
    n2 = 2 * n
    nb = n // PARTS
    own = blk * BATCH
    blocks = rows_hbm.shape[0]

    fetches = [
        pltpu.make_async_copy(src, dst, local_sem.at[i])
        for i, (src, dst) in enumerate(((t_hbm, t_ref), (rows_hbm, rows), (cols_hbm, cols)))
    ]
    for fetch in fetches:
        fetch.start()

    barrier = pltpu.get_barrier_semaphore()
    for where in (*sides, partner):
        pl.semaphore_signal(barrier, inc=1, device_id=where, device_id_type=MESH)
    loop(
        1,
        groups,
        lambda k: pl.semaphore_signal(
            barrier, inc=1, device_id={"clus": clus ^ k}, device_id_type=MESH
        ),
    )

    group_at = lax.broadcasted_iota(jnp.int32, (groups, 128), 0)
    place_at = lax.broadcasted_iota(jnp.int32, (groups, 128), 1)
    wanted = jnp.zeros((groups, 128), jnp.int32)
    for b in range(blocks):
        before = jnp.int32(0)
        for e in range(b):
            before = before + (target[e] == target[b]).astype(jnp.int32)
        position[b] = jnp.minimum(before, 1)
        hit = (group_at == target[b]) & (place_at == before)
        wanted = jnp.where(hit, col_leaf[b], wanted)
    for g in range(groups):
        want[g] = wanted[g : g + 1]

    def ask(k):
        return remote(
            want.at[clus ^ k], asked_v.at[clus], ask_send.at[k], ask_recv.at[k], {"clus": clus ^ k}
        )

    mine = pltpu.make_async_copy(want.at[clus], asked_v.at[clus], local_sem.at[3])
    learn = pltpu.make_async_copy(asked_v, asked, local_sem.at[4])

    def piece(part, z, c, u):
        return basis[part].at[pl.ds((z * 2 + c) * BATCH + u * (BATCH // SUBS), BATCH // SUBS)]

    def source(side, hop):
        return lax.rem(chip + (chips - hop if side == 0 else hop), chips)

    def ring(part, side, hop, u, arriving):
        at = piece(part, source(side, hop if arriving else hop - 1), core, u)
        i = ((part * 2 + side) * HOPS + hop - 1) * SUBS + u
        return remote(at, at, ring_send.at[i], ring_recv.at[i], sides[side])

    def pair(part, side, hop, u, arriving):
        at = piece(part, source(side, hop), 1 - core if arriving else core, u)
        i = ((part * 2 + side) * (HOPS + 1) + hop) * SUBS + u
        return remote(at, at, pair_send.at[i], pair_recv.at[i], partner)

    def travels(side, hop, u):
        return hop < HOPS or (hop == HOPS and u == side)

    def launch(part):
        for u in range(SUBS):
            for side in range(2):
                ring(part, side, 1, u, False).start()
            pair(part, 0, 0, u, False).start()

    def arrive(part, hop, u):
        for side in range(2):
            if travels(side, hop, u):
                ring(part, side, hop, u, True).wait_recv()
                if travels(side, hop + 1, u):
                    ring(part, side, hop + 1, u, False).start()
                pair(part, side, hop, u, False).start()

    arrivals = [
        (hop, u, side)
        for hop in range(1, HOPS + 1)
        for u in range(SUBS)
        for side in range(2)
        if travels(side, hop, u)
    ]

    def slot_copy(part, k):
        return remote(
            serve.at[part, k],
            slots[part].at[clus],
            slot_send.at[part, k],
            slot_recv.at[part, k],
            {"clus": clus ^ k},
        )

    def prepare():
        mine.wait()
        loop(1, groups, lambda k: ask(k).wait_recv())
        learn.start()

    def answer(part):
        for u in range(SUBS):
            pair(part, 0, 0, u, True).wait_recv()
        for hop, u, side in arrivals:
            pair(part, side, hop, u, True).wait_recv()
        if part == 0:
            learn.wait()

        def give(k):
            for c in range(2):
                serve[part, k, c] = basis[part][asked[clus ^ k, 0, c]]
            slot_copy(part, k).start()

        loop(1, groups, give)
        for c in range(2):
            slots[part][clus, c] = basis[part][asked[clus, 0, c]]

    events = []
    at = FIRST_US
    for low in range(0, PARTS, GROUP):
        group = range(low, low + GROUP)
        for hop in range(1, HOPS + 1):
            for part in group:
                for u in range(SUBS if hop < HOPS else 1):
                    at += HOP_US
                    if hop < HOPS:
                        events.append((at, lambda part=part, hop=hop, u=u: arrive(part, hop, u)))
                    else:
                        events.append(
                            (at, lambda part=part: [arrive(part, HOPS, u) for u in range(SUBS)])
                        )
            if low == 0 and hop == 2:
                events.append((at, prepare))
            if hop == HOPS - 1 and low + GROUP < PARTS:
                events.append((at, lambda low=low: [launch(low + GROUP + g) for g in range(GROUP)]))
        for part in group:
            events.append((at + 1.0, lambda part=part: answer(part)))
    clock = [None]

    def tick(step):
        if clock[0] is None:
            return
        clock[0] += step
        while events and events[0][0] <= clock[0]:
            events.pop(0)[1]()

    for m in range(BATCH):
        a = a_ref[m]
        put(work_leaf, 0, m * n, dot(a, a, 0, 0))
        put(work_leaf, n // 128, m * n, eye(n))

    def leaf_rows(part):
        for m in range(BATCH):
            xh, xl = split2(columns(work_leaf, [1], m * n + part * nb, nb))
            a = a_ref[m]
            basis[part][own + m] = (dot(xh, a, 1, 1) + dot(xl, a, 1, 1)).astype(BF16)
        if 0 < part < GROUP:
            launch(part)
        if part == 0:
            pl.semaphore_wait(barrier, groups + 2)
            launch(0)
            mine.start()
            loop(1, groups, lambda k: ask(k).start())
            clock[0] = 0.0

    factor(work_leaf, n, nb, lambda: tick(LEAF_TICK), leaf_rows)
    fetches[0].wait()
    for m in range(BATCH):
        uh, ul = split2(upper(columns(work_leaf, [0], m * n, n)))
        th, tl = split2(t_ref[m])
        st = dot(jnp.concatenate([uh, ul], axis=1), jnp.concatenate([th, th], axis=0), 1, 0)
        st = st + dot(uh, tl, 1, 0)
        stacked[m] = st
        stacked_send[m] = st.astype(BF16)
    swap = remote(stacked_send, stacked_recv, stack_sem.at[0], stack_sem.at[1], partner)
    swap.start()
    tick(1.0)

    swap.wait_recv()
    tick(1.0)
    for m in range(BATCH):
        sh, sl = split2(stacked[m])
        p = stacked_recv[(m + BATCH // 2) % BATCH]
        g = dot(jnp.concatenate([sh, sl], axis=0), jnp.concatenate([sh, sh], axis=0), 0, 0)
        g = g + dot(jnp.concatenate([sh, p], axis=0), jnp.concatenate([sl, p], axis=0), 0, 0)
        put(work_parent, 0, m * n2, g)
        put(work_parent, n2 // 128, m * n2, eye(n2))
    tick(1.5)
    factor(work_parent, n2, 32, lambda: tick(PARENT_TICK), lambda number: None)
    for m in range(BATCH):
        sh, sl = split2(stacked[m])
        xh, xl = split2(columns(work_parent, range(2, 4), m * n2, n2))
        new_ref[m] = dot(sh, xh, 1, 1) + (dot(sh, xl, 1, 1) + dot(sl, xh, 1, 1))
    while events:
        events.pop(0)[1]()

    for fetch in fetches[1:]:
        fetch.wait()

    def near_step(i):
        for j in range(4):
            b = i * 4 + j
            lhs = jnp.concatenate([basis[part][row_leaf[b]] for part in range(PARTS)], axis=0)
            value = dot(lhs, rows[b], 1, 1)
            live = lax.broadcasted_iota(jnp.int32, value.shape, 1) < rank[b] * SLAB
            near[b] = jnp.where(live, value, 0.0).astype(BF16)

    loop(0, blocks // 4, near_step)

    def far_step(i, low):
        for j in range(4):
            b = i * 4 + j
            g, c = target[b], position[b]
            parts = range(low, low + FINISH)
            lhs = jnp.concatenate([slots[part][g, c] for part in parts], axis=0)
            far = dot(lhs, cols[b], 1, 1).astype(BF16)
            out_ref[b, :, low * nb : (low + FINISH) * nb] = dot(near[b], far, 1, 1)

    for low in range(0, PARTS, FINISH):
        for part in range(low, low + FINISH):
            loop(1, groups, lambda k, part=part: slot_copy(part, k).wait_recv())
        loop(0, blocks // 4, lambda i, low=low: far_step(i, low))

    for part in range(PARTS):
        for u in range(SUBS):
            for side in range(2):
                for hop in range(1, HOPS + 1):
                    if travels(side, hop, u):
                        ring(part, side, hop, u, False).wait_send()
            pair(part, 0, 0, u, False).wait_send()
        for hop, u, side in arrivals:
            pair(part, side, hop, u, False).wait_send()
    swap.wait_send()

    def drain(k):
        ask(k).wait_send()
        for part in range(PARTS):
            slot_copy(part, k).wait_send()

    loop(1, groups, drain)


def whole(row_leaf, target, col_leaf, rank, leaf_basis, transfer, rows, cols):
    groups, width = lax.axis_size("clus"), lax.axis_size("blk")
    count, points, n = leaf_basis.shape
    blocks, rank_max = rows.shape[0], rows.shape[1]
    smem, vmem = pltpu.SMEM, pltpu.VMEM
    dma = pltpu.SemaphoreType.DMA
    leaves = count * width
    rings, pairs = PARTS * 2 * HOPS * SUBS, PARTS * 2 * (HOPS + 1) * SUBS
    return pl.pallas_call(
        whole_kernel,
        out_shape=(
            jax.ShapeDtypeStruct((blocks, n, n), F32),
            jax.ShapeDtypeStruct(transfer.shape, F32),
        ),
        in_specs=[pl.BlockSpec(memory_space=smem)] * 4
        + [pl.BlockSpec(memory_space=vmem)]
        + [pl.BlockSpec(memory_space=pl.ANY)] * 3,
        out_specs=(pl.BlockSpec(memory_space=vmem), pl.BlockSpec(memory_space=vmem)),
        scratch_shapes=[
            vmem((2, count * n, 128), F32),
            vmem((4, count * 2 * n, 128), F32),
            vmem(transfer.shape, F32),
            vmem(transfer.shape, BF16),
            vmem(transfer.shape, BF16),
            vmem((PARTS, groups, 2, n // PARTS, points), BF16),
            vmem(transfer.shape, F32),
            vmem(rows.shape, BF16),
            vmem(cols.shape, BF16),
            vmem((blocks, n, rank_max), BF16),
            vmem((groups, 1, 128), jnp.int32),
            vmem((groups, 1, 128), jnp.int32),
            smem((groups, 1, 128), jnp.int32),
            smem((blocks,), jnp.int32),
            dma((rings,)),
            dma((rings,)),
            dma((pairs,)),
            dma((pairs,)),
            dma((2,)),
            dma((groups,)),
            dma((groups,)),
            dma((PARTS, groups)),
            dma((PARTS, groups)),
            dma((5,)),
            *[vmem((leaves, n // PARTS, points), BF16)] * PARTS,
            *[vmem((groups, 2, n // PARTS, points), BF16)] * PARTS,
        ],
        compiler_params=pltpu.CompilerParams(
            collective_id=0, has_side_effects=True, vmem_limit_bytes=60 * 2**20
        ),
        name="whole",
    )(row_leaf, target, col_leaf, rank, leaf_basis, transfer, rows, cols)


def per_device(
    leaf_basis, transfer, block_rows, block_cols, rank_slabs, row_leaf, col_group, col_leaf
):
    return whole(
        row_leaf,
        col_group[:, 0],
        col_leaf,
        rank_slabs,
        leaf_basis,
        transfer,
        jnp.swapaxes(block_rows, 1, 2),
        jnp.swapaxes(block_cols, 1, 2),
    )


def solution(mesh):
    placed = (
        P(("clus", "blk"), None, None),
        P(("clus", "blk"), None, None),
        P(("clus", "blk"), None, None),
        P(("clus", "blk"), None, None),
        P(("clus", "blk")),
        P(("clus", "blk")),
        P(("clus", "blk"), None),
        P(("clus", "blk")),
    )
    return jax.shard_map(
        per_device,
        mesh=mesh,
        in_specs=placed,
        out_specs=(P(("clus", "blk"), None, None), P(("clus", "blk"), None, None)),
        check_vma=False,
    )
```

```python
import jax
import jax.numpy as jnp
from jax import lax
from jax.experimental import pallas as pl
from jax.experimental.pallas import tpu as pltpu
from jax.sharding import PartitionSpec as P

SLAB = 64
F32, BF16 = jnp.float32, jnp.bfloat16
BATCH = 8
PANEL = 8


def split2(x):
    hi = x.astype(BF16)
    return hi, (x - hi.astype(F32)).astype(BF16)


def dot(a, b, ca, cb):
    return lax.dot_general(a, b, (((ca,), (cb,)), ((), ())), preferred_element_type=F32)


def lane(row, j):
    part = row[j // 128]
    return jnp.broadcast_to(part[:, j % 128 : j % 128 + 1], (BATCH, 128))


def factor_block(rows, first, tick):
    count = len(rows)
    for base in range(0, count, PANEL):
        s = {}
        for i in range(PANEL):
            for j in range(i, PANEL):
                s[i, j] = lane(rows[base + i], first + base + j)
        for k in range(PANEL):
            d = lax.rsqrt(s[k, k])
            for j in range(k + 1, PANEL):
                s[k, j] = s[k, j] * d
            for i in range(k + 1, PANEL):
                for j in range(i, PANEL):
                    s[i, j] = s[i, j] - s[k, i] * s[k, j]
            rows[base + k] = {t: v * d for t, v in rows[base + k].items()}
            for i in range(k + 1, PANEL):
                rows[base + i] = {
                    t: v - s[k, i] * rows[base + k][t] for t, v in rows[base + i].items()
                }
        for i in range(base + PANEL, count):
            row = dict(rows[i])
            for k in range(PANEL):
                m = lane(rows[base + k], first + i)
                for t in row:
                    row[t] = row[t] - m * rows[base + k][t]
            rows[i] = row
        tick()
    return rows


def columns(work, span, start, count):
    return jnp.concatenate([work[t, start : start + count, :] for t in span], axis=1)


def put(work, first, start, value):
    for t in range(value.shape[1] // 128):
        work[first + t, start : start + value.shape[0], :] = value[:, t * 128 : (t + 1) * 128]


def factor(work, n, nb, tick, after_block):
    tiles = n // 128
    for first in range(0, n, nb):
        t0 = first // 128
        live = list(range(t0, tiles)) + [tiles + t for t in range(t0 + 1)]
        rows = []
        for i in range(first, first + nb):
            rows.append({t: work[t, pl.ds(i, BATCH, stride=n), :] for t in live})
        rows = factor_block(rows, first, tick)
        for i in range(nb):
            for t in live:
                work[t, pl.ds(first + i, BATCH, stride=n), :] = rows[i][t]
        after_block(first // nb)
        rest = first + nb
        if rest < n:
            r0 = rest // 128
            span = list(range(r0, tiles)) + [tiles + t for t in range(t0 + 1)]
            skip = rest - r0 * 128
            for m in range(BATCH):
                hi, lo = split2(columns(work, span, m * n + first, nb))
                lhs = jnp.concatenate([hi, lo, hi], axis=0)[:, 0 : n - r0 * 128]
                rhs = jnp.concatenate([hi, hi, lo], axis=0)
                upd = dot(lhs, rhs, 0, 0)
                for at, t in enumerate(span):
                    work[t, m * n + rest : (m + 1) * n, :] = (
                        work[t, m * n + rest : (m + 1) * n, :] - upd[skip:, at * 128 : (at + 1) * 128]
                    )


def eye(n):
    return (lax.broadcasted_iota(jnp.int32, (n, n), 0) == lax.broadcasted_iota(jnp.int32, (n, n), 1)).astype(F32)


def upper(x):
    n = x.shape[0]
    return jnp.where(
        lax.broadcasted_iota(jnp.int32, (n, n), 0) <= lax.broadcasted_iota(jnp.int32, (n, n), 1), x, 0.0
    )


MESH = pl.DeviceIdType.MESH
PARTS = 4
SUBS = 4
HOPS = 4
LEAF_TICK, PARENT_TICK = 0.5, 0.48
HOP_US, FIRST_US = 0.35, 0.8
GROUP = 2
FINISH = 2


def remote(src, dst, send, recv, where):
    return pltpu.make_async_remote_copy(
        src_ref=src, dst_ref=dst, send_sem=send, recv_sem=recv, device_id=where, device_id_type=MESH
    )


def loop(low, high, step):
    def body(i, carry):
        step(i)
        return carry

    lax.fori_loop(low, high, body, 0)


def whole_kernel(
    row_leaf, target, col_leaf, rank,
    a_ref, t_hbm, rows_hbm, cols_hbm,
    out_ref, new_ref,
    work_leaf, work_parent, stacked, stacked_send, stacked_recv, serve,
    t_ref, rows, cols, near, want, asked_v, asked, position,
    ring_send, ring_recv, pair_send, pair_recv, stack_sem, ask_send, ask_recv, slot_send, slot_recv,
    local_sem, *parted,
):
    basis, slots = parted[:PARTS], parted[PARTS:]
    clus, blk = lax.axis_index("clus"), lax.axis_index("blk")
    groups, width = lax.axis_size("clus"), lax.axis_size("blk")
    chips = width // 2
    core, chip = lax.rem(blk, 2), lax.div(blk, 2)
    sides = (
        {"blk": lax.rem(chip + 1, chips) * 2 + core},
        {"blk": lax.rem(chip + chips - 1, chips) * 2 + core},
    )
    partner = {"blk": chip * 2 + 1 - core}
    n = a_ref.shape[2]
    n2 = 2 * n
    nb = n // PARTS
    own = blk * BATCH
    blocks = rows_hbm.shape[0]

    fetches = [
        pltpu.make_async_copy(src, dst, local_sem.at[i])
        for i, (src, dst) in enumerate(((t_hbm, t_ref), (rows_hbm, rows), (cols_hbm, cols)))
    ]
    for fetch in fetches:
        fetch.start()

    barrier = pltpu.get_barrier_semaphore()
    for where in (*sides, partner):
        pl.semaphore_signal(barrier, inc=1, device_id=where, device_id_type=MESH)
    loop(
        1,
        groups,
        lambda k: pl.semaphore_signal(
            barrier, inc=1, device_id={"clus": clus ^ k}, device_id_type=MESH
        ),
    )

    group_at = lax.broadcasted_iota(jnp.int32, (groups, 128), 0)
    place_at = lax.broadcasted_iota(jnp.int32, (groups, 128), 1)
    wanted = jnp.zeros((groups, 128), jnp.int32)
    for b in range(blocks):
        before = jnp.int32(0)
        for e in range(b):
            before = before + (target[e] == target[b]).astype(jnp.int32)
        position[b] = jnp.minimum(before, 1)
        hit = (group_at == target[b]) & (place_at == before)
        wanted = jnp.where(hit, col_leaf[b], wanted)
    for g in range(groups):
        want[g] = wanted[g : g + 1]

    def ask(k):
        return remote(
            want.at[clus ^ k], asked_v.at[clus], ask_send.at[k], ask_recv.at[k], {"clus": clus ^ k}
        )

    mine = pltpu.make_async_copy(want.at[clus], asked_v.at[clus], local_sem.at[3])
    learn = pltpu.make_async_copy(asked_v, asked, local_sem.at[4])

    def piece(part, z, c, u):
        return basis[part].at[pl.ds((z * 2 + c) * BATCH + u * (BATCH // SUBS), BATCH // SUBS)]

    def source(side, hop):
        return lax.rem(chip + (chips - hop if side == 0 else hop), chips)

    def ring(part, side, hop, u, arriving):
        at = piece(part, source(side, hop if arriving else hop - 1), core, u)
        i = ((part * 2 + side) * HOPS + hop - 1) * SUBS + u
        return remote(at, at, ring_send.at[i], ring_recv.at[i], sides[side])

    def pair(part, side, hop, u, arriving):
        at = piece(part, source(side, hop), 1 - core if arriving else core, u)
        i = ((part * 2 + side) * (HOPS + 1) + hop) * SUBS + u
        return remote(at, at, pair_send.at[i], pair_recv.at[i], partner)

    def travels(side, hop, u):
        return hop < HOPS or (hop == HOPS and u // (SUBS // 2) == side)

    def launch(part):
        for u in range(SUBS):
            for side in range(2):
                ring(part, side, 1, u, False).start()
            pair(part, 0, 0, u, False).start()

    def arrive(part, hop, u):
        for side in range(2):
            if travels(side, hop, u):
                ring(part, side, hop, u, True).wait_recv()
                if travels(side, hop + 1, u):
                    ring(part, side, hop + 1, u, False).start()
                pair(part, side, hop, u, False).start()

    arrivals = [
        (hop, u, side)
        for hop in range(1, HOPS + 1)
        for u in range(SUBS)
        for side in range(2)
        if travels(side, hop, u)
    ]

    def slot_copy(part, k):
        return remote(
            serve.at[part, k],
            slots[part].at[clus],
            slot_send.at[part, k],
            slot_recv.at[part, k],
            {"clus": clus ^ k},
        )

    def prepare():
        mine.wait()
        loop(1, groups, lambda k: ask(k).wait_recv())
        learn.start()

    def answer(part):
        for u in range(SUBS):
            pair(part, 0, 0, u, True).wait_recv()
        for hop, u, side in arrivals:
            pair(part, side, hop, u, True).wait_recv()
        if part == 0:
            learn.wait()

        def give(k):
            for c in range(2):
                serve[part, k, c] = basis[part][asked[clus ^ k, 0, c]]
            slot_copy(part, k).start()

        loop(1, groups, give)
        for c in range(2):
            slots[part][clus, c] = basis[part][asked[clus, 0, c]]

    events = []
    at = FIRST_US
    for low in range(0, PARTS, GROUP):
        group = range(low, low + GROUP)
        for hop in range(1, HOPS + 1):
            for part in group:
                for u in range(SUBS if hop < HOPS else 1):
                    at += HOP_US
                    if hop < HOPS:
                        events.append((at, lambda part=part, hop=hop, u=u: arrive(part, hop, u)))
                    else:
                        events.append(
                            (at, lambda part=part: [arrive(part, HOPS, u) for u in range(SUBS)])
                        )
            if low == 0 and hop == 2:
                events.append((at, prepare))
            if hop == HOPS - 1 and low + GROUP < PARTS:
                events.append((at, lambda low=low: [launch(low + GROUP + g) for g in range(GROUP)]))
        for part in group:
            events.append((at + 1.0, lambda part=part: answer(part)))
    clock = [None]

    def tick(step):
        if clock[0] is None:
            return
        clock[0] += step
        while events and events[0][0] <= clock[0]:
            events.pop(0)[1]()

    for m in range(BATCH):
        a = a_ref[m]
        put(work_leaf, 0, m * n, dot(a, a, 0, 0))
        put(work_leaf, n // 128, m * n, eye(n))

    def leaf_rows(part):
        for m in range(BATCH):
            xh, xl = split2(columns(work_leaf, [1], m * n + part * nb, nb))
            a = a_ref[m]
            basis[part][own + m] = (dot(xh, a, 1, 1) + dot(xl, a, 1, 1)).astype(BF16)
        if 0 < part < GROUP:
            launch(part)
        if part == 0:
            pl.semaphore_wait(barrier, groups + 2)
            launch(0)
            mine.start()
            loop(1, groups, lambda k: ask(k).start())
            clock[0] = 0.0

    factor(work_leaf, n, nb, lambda: tick(LEAF_TICK), leaf_rows)
    fetches[0].wait()
    for m in range(BATCH):
        uh, ul = split2(upper(columns(work_leaf, [0], m * n, n)))
        th, tl = split2(t_ref[m])
        st = dot(jnp.concatenate([uh, ul], axis=1), jnp.concatenate([th, th], axis=0), 1, 0)
        st = st + dot(uh, tl, 1, 0)
        stacked[m] = st
        stacked_send[m] = st.astype(BF16)
    swap = remote(stacked_send, stacked_recv, stack_sem.at[0], stack_sem.at[1], partner)
    swap.start()
    tick(1.0)

    swap.wait_recv()
    tick(1.0)
    for m in range(BATCH):
        sh, sl = split2(stacked[m])
        p = stacked_recv[(m + BATCH // 2) % BATCH]
        g = dot(jnp.concatenate([sh, sl], axis=0), jnp.concatenate([sh, sh], axis=0), 0, 0)
        g = g + dot(jnp.concatenate([sh, p], axis=0), jnp.concatenate([sl, p], axis=0), 0, 0)
        put(work_parent, 0, m * n2, g)
        put(work_parent, n2 // 128, m * n2, eye(n2))
    tick(1.5)
    factor(work_parent, n2, 32, lambda: tick(PARENT_TICK), lambda number: None)
    for m in range(BATCH):
        sh, sl = split2(stacked[m])
        xh, xl = split2(columns(work_parent, range(2, 4), m * n2, n2))
        new_ref[m] = dot(sh, xh, 1, 1) + (dot(sh, xl, 1, 1) + dot(sl, xh, 1, 1))
    while events:
        events.pop(0)[1]()

    for fetch in fetches[1:]:
        fetch.wait()

    def near_step(i):
        for j in range(4):
            b = i * 4 + j
            lhs = jnp.concatenate([basis[part][row_leaf[b]] for part in range(PARTS)], axis=0)
            value = dot(lhs, rows[b], 1, 1)
            live = lax.broadcasted_iota(jnp.int32, value.shape, 1) < rank[b] * SLAB
            near[b] = jnp.where(live, value, 0.0).astype(BF16)

    loop(0, blocks // 4, near_step)

    def far_step(i, low):
        for j in range(4):
            b = i * 4 + j
            g, c = target[b], position[b]
            parts = range(low, low + FINISH)
            lhs = jnp.concatenate([slots[part][g, c] for part in parts], axis=0)
            far = dot(lhs, cols[b], 1, 1).astype(BF16)
            out_ref[b, :, low * nb : (low + FINISH) * nb] = dot(near[b], far, 1, 1)

    for low in range(0, PARTS, FINISH):
        for part in range(low, low + FINISH):
            loop(1, groups, lambda k, part=part: slot_copy(part, k).wait_recv())
        loop(0, blocks // 4, lambda i, low=low: far_step(i, low))

    for part in range(PARTS):
        for u in range(SUBS):
            for side in range(2):
                for hop in range(1, HOPS + 1):
                    if travels(side, hop, u):
                        ring(part, side, hop, u, False).wait_send()
            pair(part, 0, 0, u, False).wait_send()
        for hop, u, side in arrivals:
            pair(part, side, hop, u, False).wait_send()
    swap.wait_send()

    def drain(k):
        ask(k).wait_send()
        for part in range(PARTS):
            slot_copy(part, k).wait_send()

    loop(1, groups, drain)


def whole(row_leaf, target, col_leaf, rank, leaf_basis, transfer, rows, cols):
    groups, width = lax.axis_size("clus"), lax.axis_size("blk")
    count, points, n = leaf_basis.shape
    blocks, rank_max = rows.shape[0], rows.shape[1]
    smem, vmem = pltpu.SMEM, pltpu.VMEM
    dma = pltpu.SemaphoreType.DMA
    leaves = count * width
    rings, pairs = PARTS * 2 * HOPS * SUBS, PARTS * 2 * (HOPS + 1) * SUBS
    return pl.pallas_call(
        whole_kernel,
        out_shape=(
            jax.ShapeDtypeStruct((blocks, n, n), F32),
            jax.ShapeDtypeStruct(transfer.shape, F32),
        ),
        in_specs=[pl.BlockSpec(memory_space=smem)] * 4
        + [pl.BlockSpec(memory_space=vmem)]
        + [pl.BlockSpec(memory_space=pl.ANY)] * 3,
        out_specs=(pl.BlockSpec(memory_space=vmem), pl.BlockSpec(memory_space=vmem)),
        scratch_shapes=[
            vmem((2, count * n, 128), F32),
            vmem((4, count * 2 * n, 128), F32),
            vmem(transfer.shape, F32),
            vmem(transfer.shape, BF16),
            vmem(transfer.shape, BF16),
            vmem((PARTS, groups, 2, n // PARTS, points), BF16),
            vmem(transfer.shape, F32),
            vmem(rows.shape, BF16),
            vmem(cols.shape, BF16),
            vmem((blocks, n, rank_max), BF16),
            vmem((groups, 1, 128), jnp.int32),
            vmem((groups, 1, 128), jnp.int32),
            smem((groups, 1, 128), jnp.int32),
            smem((blocks,), jnp.int32),
            dma((rings,)),
            dma((rings,)),
            dma((pairs,)),
            dma((pairs,)),
            dma((2,)),
            dma((groups,)),
            dma((groups,)),
            dma((PARTS, groups)),
            dma((PARTS, groups)),
            dma((5,)),
            *[vmem((leaves, n // PARTS, points), BF16)] * PARTS,
            *[vmem((groups, 2, n // PARTS, points), BF16)] * PARTS,
        ],
        compiler_params=pltpu.CompilerParams(
            collective_id=0, has_side_effects=True, vmem_limit_bytes=60 * 2**20
        ),
        name="whole",
    )(row_leaf, target, col_leaf, rank, leaf_basis, transfer, rows, cols)


def per_device(
    leaf_basis, transfer, block_rows, block_cols, rank_slabs, row_leaf, col_group, col_leaf
):
    return whole(
        row_leaf,
        col_group[:, 0],
        col_leaf,
        rank_slabs,
        leaf_basis,
        transfer,
        jnp.swapaxes(block_rows, 1, 2),
        jnp.swapaxes(block_cols, 1, 2),
    )


def solution(mesh):
    placed = (
        P(("clus", "blk"), None, None),
        P(("clus", "blk"), None, None),
        P(("clus", "blk"), None, None),
        P(("clus", "blk"), None, None),
        P(("clus", "blk")),
        P(("clus", "blk")),
        P(("clus", "blk"), None),
        P(("clus", "blk")),
    )
    return jax.shard_map(
        per_device,
        mesh=mesh,
        in_specs=placed,
        out_specs=(P(("clus", "blk"), None, None), P(("clus", "blk"), None, None)),
        check_vma=False,
    )
```
